512 devices in a mesh: grp: 8 (over y), tm: 64 (over z, x, core).
Axes of the slice: x: 4, y: 8, z: 8, core: 2. Of those that a mesh axis runs over, the one named last changes fastest.
Arguments:
- audio_rows: bfloat16 [131072, 1024], P(('grp', 'tm')), may hold values from -6 to 6
- routing: int32 [131072, 1], P(('grp', 'tm')), may hold values from 0 to 63; in each aligned block of 256 rows (0 to 255, 256 to 511, ...) at most 8 rows name the same one
- row_band: int32 [131072], P(('grp', 'tm')), may hold values from 0 to 3
- block_band: int32 [512], P(('grp', 'tm')), may hold values from 0 to 3
- latents: bfloat16 [65536, 1024], P(('grp', 'tm')), may hold values from -480 to 480
- kv_weight: bfloat16 [1024, 2048], P('tm'), may hold values from -0.1875 to 0.1875
- null_key: float32 [1024], replicated, may hold values from -6 to 6
- null_value: float32 [1024], replicated, may hold values from -6 to 6
- out_weight: bfloat16 [1024, 1024], replicated, may hold values from -0.1875 to 0.1875
- mlp_gain: float32 [1024], replicated, may hold values from 0.25 to 1.75
- up_weight: bfloat16 [1024, 8192], P('tm', 'grp'), may hold values from -0.1875 to 0.1875
- down_weight: bfloat16 [8192, 1024], P('grp', 'tm'), may hold values from -0.25 to 0.25
Outputs:
- mixed: bfloat16 [65536, 1024], P('tm', 'grp')
The draws below stay inside these ranges and needn't reach their ends.
Inputs may be any that keep to these rules, and one draw needn't show every extreme that they name: `routing`: among the rows of one device no window is named by more than 8 rows, and in some devices' rows one window is named by exactly 8.
All inputs are finite; a program needn't handle non-finite values.
Results may differ from the reference program's by a relative error of at most 0.015.
Values may be sent and summed in bfloat16 or wider, within the bound.
No kernel may reach another device: no remote copies, remote signals or barrier semaphores. Data moves between devices by JAX's collectives and lax.ppermute only.
A program may use at most 64 MiB of HBM per device.

```python
import math
import jax
import jax.numpy as jnp
import numpy as np
from jax import lax

D = 1024
DA = 1024
F = 8192
HD = 128
LAT = 128
NB = 4
A_DEV = 256
CAP = 8
BLOCKS = 512
LATENTS = 65536
AUDIO = 131072
N_GRP = 8
N_TM = 64


def draw_latents(key, part):
    base = jnp.clip(jax.random.normal(key, (LATENTS, D), jnp.float32), -6.0, 6.0)
    return base.astype(jnp.bfloat16)


def place_ends(entries, rng, low, top_value):
    longest = entries.shape.index(max(entries.shape))
    spots = []
    for shift in (0, 1):
        where = [jax.random.randint(jax.random.fold_in(rng, axis), (), 0, length) for axis, length in enumerate(entries.shape)]
        where[longest] = (where[longest] + shift) % entries.shape[longest]
        spots.append(tuple(where))
    return entries.at[spots[0]].set(low).at[spots[1]].set(top_value)


def steps_of(stream_key, dims, pieces, low, top_value):
    loudness, own = 1.0, jax.random.fold_in(stream_key, 6)
    for dim, blocks in pieces:
        draws = jnp.exp(jax.random.uniform(jax.random.fold_in(own, dim), (blocks,), jnp.float32, low / len(pieces), top_value / len(pieces)))
        loudness = loudness * jnp.repeat(draws, dims[dim] // blocks).reshape([-1 if axis == dim else 1 for axis in range(len(dims))])
    return loudness


def assign_block(own_key, own, number, rows, number_of, top, limit, skew):
    order = jax.random.permutation(own_key, number_of)
    crowded, ordinary = shares(number_of, rows * top, limit, skew, True), shares(number_of, rows * top, limit, skew, False)
    places = jnp.arange(number_of)

    def named(sizes, rotation):
        used = int((sizes > 0).sum())
        fixed = max(1, used // 4)
        moved = fixed + (places - fixed + rotation * (used - fixed)) % max(1, number_of - fixed)
        return jnp.zeros((number_of,), jnp.int32).at[order[jnp.where(places < fixed, places, moved)]].set(jnp.asarray(sizes, jnp.int32))

    sizes = jnp.where(number % 4 == 0, named(crowded, number // 4), named(ordinary, number - number // 4 - 1))
    mixed = jax.random.permutation(jax.random.fold_in(own, 3), number_of)
    donor, taker = mixed[0:number_of // 2 * 2:2], mixed[1:number_of // 2 * 2:2]
    room = jnp.minimum(sizes[donor] - 1, limit - sizes[taker]) // 2
    room = jnp.where((donor == order[0]) | (taker == order[0]) | (sizes[taker] == 0), 0, jnp.maximum(room, 0))
    moved = jax.random.randint(jax.random.fold_in(own, 4), (number_of // 2,), 0, 1 << 20) % (room + 1)
    sizes = sizes.at[donor].add(-moved).at[taker].add(moved)
    labels = jnp.searchsorted(jnp.cumsum(sizes), jnp.arange(rows * top), side="right").astype(jnp.int32)
    table = labels.reshape(top, rows).T
    table = table[jax.random.permutation(jax.random.fold_in(own, 1), rows)]
    rotation = jax.random.randint(jax.random.fold_in(own, 2), (rows, 1), 0, top)
    return jnp.take_along_axis(table, (jnp.arange(top)[None, :] + rotation) % top, axis=1)


def shares(number_of, total, limit, slope, full):
    weights = [(1 << 20) // math.isqrt(grade ** slope) + 1 for grade in range(1, number_of + 1)]
    largest = limit if full else min(limit, max(-(-total // number_of), total * weights[0] // sum(weights)))
    least = 1 if total - largest >= number_of - 1 else 0
    counts, surplus = [largest] + [least] * (number_of - 1), total - largest - least * (number_of - 1)
    while surplus > 0:
        candidates = [i for i in range(1, number_of) if counts[i] < largest] or [i for i in range(1, number_of) if counts[i] < limit]
        whole, budget = sum([weights[i] for i in candidates]), surplus
        for i in candidates:
            extra = min(limit - counts[i], max(1, budget * weights[i] // whole), surplus)
            counts[i] = counts[i] + extra
            surplus = surplus - extra
    return np.array(counts)


def normal_values(own_key, shape, scale, limit, split=(), kind=jnp.bfloat16):
    result = scale * jax.random.normal(own_key, shape, jnp.float32)
    if split:
        result = result * steps_of(own_key, shape, split, -0.22, 0.18)
    return jnp.clip(result, -limit, limit).astype(kind)


def setup_inputs(seed: int = 0) -> dict:
    splits = jax.random.split(jax.random.key(seed), 13)
    audio_rows = normal_values(splits[0], (AUDIO, DA), 1.0, 6.0, ((0, 512),))
    routing_keys = jax.random.split(jax.random.fold_in(splits[1], 1), AUDIO // A_DEV)
    routing_turns = jax.random.permutation(jax.random.fold_in(splits[1], 3), AUDIO // A_DEV)
    routing = jax.vmap(lambda own, number: assign_block(jax.random.fold_in(splits[1], 2), own, number, A_DEV, N_TM, 1, CAP, 2))(routing_keys, routing_turns).reshape((AUDIO, 1))
    row_band = place_ends(jax.random.randint(splits[2], (AUDIO,), 0, NB), jax.random.fold_in(splits[2], 1), 0, NB - 1).astype(jnp.int32)
    block_band = place_ends(jax.random.randint(splits[3], (BLOCKS,), 0, NB), jax.random.fold_in(splits[3], 1), 0, NB - 1).astype(jnp.int32)
    latents = draw_latents(jax.random.fold_in(splits[12], 71), 0)
    kv_weight = normal_values(splits[5], (DA, 2 * D), DA ** -0.5, 0.1875, ((0, 64),))
    null_key = normal_values(splits[6], (D,), 1.0, 6.0, (), jnp.float32)
    null_value = normal_values(splits[7], (D,), 1.0, 6.0, (), jnp.float32)
    out_weight = normal_values(splits[8], (D, D), D ** -0.5, 0.1875)
    mlp_gain = jnp.clip(1.0 + 0.15 * jax.random.normal(splits[9], (D,), jnp.float32), 0.25, 1.75)
    up_weight = normal_values(splits[10], (D, F), D ** -0.5, 0.1875, ((0, 64), (1, 8)))
    down_weight = normal_values(splits[11], (F, D), (F // 16) ** -0.5, 0.25, ((0, 8), (1, 64)))
    return dict(audio_rows=audio_rows, routing=routing, row_band=row_band, block_band=block_band, latents=latents, kv_weight=kv_weight, null_key=null_key, null_value=null_value, out_weight=out_weight, mlp_gain=mlp_gain, up_weight=up_weight, down_weight=down_weight)


def slot_numbers(destination):
    blocked = destination.reshape(N_GRP * N_TM, A_DEV)
    onehot = (blocked[:, :, None] == jnp.arange(N_TM, dtype=jnp.int32)[None, None, :]).astype(jnp.int32)
    earlier = jnp.cumsum(onehot, axis=1) - onehot
    return lax.optimization_barrier(jnp.sum(earlier * onehot, axis=2)).astype(jnp.int32).reshape(-1)

def attend(queries, kv_slots, usable, null_key, null_value):
    count = queries.shape[0]
    slots = kv_slots.shape[0]
    width = queries.shape[1]
    heads = width // HD
    scale = 1.0 / float(HD) ** 0.5
    query = queries.astype(jnp.float32).reshape(count, heads, HD)
    keyset = kv_slots[:, :width].astype(jnp.float32).reshape(slots, heads, HD)
    valset = kv_slots[:, width:].astype(jnp.float32).reshape(slots, heads, HD)
    scores = jnp.einsum('lhd,shd->hls', query, keyset) * scale
    null_scores = jnp.einsum('lhd,hd->hl', query, null_key.reshape(heads, HD)) * scale
    masked = jnp.where(usable[None, None, :], scores, -1e+30)
    highest = jnp.maximum(lax.optimization_barrier(jnp.max(masked, axis=-1)), null_scores)
    expo = jnp.where(usable[None, None, :], jnp.exp(masked - highest[:, :, None]), 0.0)
    null_expo = jnp.exp(null_scores - highest)
    denom = lax.optimization_barrier(jnp.sum(expo, axis=-1)) + null_expo
    weights = (expo / denom[:, :, None]).astype(jnp.bfloat16)
    null_weights = (null_expo / denom).astype(jnp.bfloat16)
    summed = jnp.einsum('hls,shd->lhd', weights.astype(jnp.float32), valset)
    summed = summed + jnp.transpose(null_weights.astype(jnp.float32))[:, :, None] * null_value.reshape(heads, HD)[None, :, :]
    return summed.reshape(count, width).astype(jnp.bfloat16)

def layer_norm(window, mlp_gain):
    values = window.astype(jnp.float32)
    center = values - lax.optimization_barrier(jnp.mean(values, axis=-1, keepdims=True))
    spread = lax.optimization_barrier(jnp.mean(center * center, axis=-1, keepdims=True))
    return (center * lax.rsqrt(spread + 1e-05) * mlp_gain).astype(jnp.bfloat16)

def reference(audio_rows, routing, row_band, block_band, latents, kv_weight, null_key, null_value, out_weight, mlp_gain, up_weight, down_weight):
    destination = routing[:, 0].astype(jnp.int32)
    slot_index = slot_numbers(destination)
    keys_vals = jnp.dot(audio_rows, kv_weight, preferred_element_type=jnp.float32).astype(jnp.bfloat16)
    row_ids = jnp.arange(AUDIO, dtype=jnp.int32)
    device_of = row_ids // A_DEV
    group_of = device_of // N_TM
    source_of = device_of % N_TM
    block_of = group_of * N_TM + destination
    index_table = jnp.full((N_GRP * N_TM, N_TM, CAP), AUDIO, jnp.int32).at[block_of, source_of, slot_index].set(row_ids)
    kv_padded = jnp.concatenate([keys_vals, jnp.zeros((1, 2 * D), jnp.bfloat16)], axis=0)
    band_padded = jnp.concatenate([row_band.astype(jnp.int32), jnp.full((1,), -4, jnp.int32)], axis=0)
    latent_blocks = latents.reshape(N_GRP * N_TM, LAT, D)

    def one_block(packed):
        table, queries, band_here = packed
        flat_index = table.reshape(-1)
        kv_slots = kv_padded[flat_index]
        usable = jnp.abs(band_padded[flat_index] - band_here) <= 1
        attended = attend(queries, kv_slots, usable, null_key, null_value)
        return (queries.astype(jnp.float32) + jnp.dot(attended, out_weight, preferred_element_type=jnp.float32)).astype(jnp.bfloat16)
    joined = lax.map(one_block, (index_table, latent_blocks, block_band.astype(jnp.int32)))
    windows = jnp.transpose(joined.reshape(N_GRP, N_TM, LAT, D), (1, 0, 2, 3)).reshape(N_TM, N_GRP * LAT, D)

    def one_window(window):
        normed = layer_norm(window, mlp_gain)
        hidden = jax.nn.gelu(jnp.dot(normed, up_weight, preferred_element_type=jnp.float32)).astype(jnp.bfloat16)
        return (window.astype(jnp.float32) + jnp.dot(hidden, down_weight, preferred_element_type=jnp.float32)).astype(jnp.bfloat16)
    mixed = lax.map(one_window, windows)
    return mixed.reshape(N_TM * N_GRP * LAT, D)
```

```python
import jax
import jax.numpy as jnp
from jax import lax
from jax.experimental import pallas as pl
from jax.experimental.pallas import tpu as pltpu
from jax.sharding import PartitionSpec as P

HD = 128
BAND_LANES = 128
BAND_SHIFT = 4
WEIGHT_SCALE = 2.0**17
JOINED_SCALE = 0.25


def pack_kernel(owners, capacity, dest_ref, band_ref, rows_ref, out_ref):
    rows = rows_ref.shape[0]
    width = rows_ref.shape[1]
    slots = owners * capacity
    dest = dest_ref[...]
    owner_ids = lax.broadcasted_iota(jnp.int32, (owners, rows), 0)
    named = (owner_ids == dest).astype(jnp.float32)
    before = lax.broadcasted_iota(jnp.int32, (rows, rows), 0) < lax.broadcasted_iota(
        jnp.int32, (rows, rows), 1
    )
    earlier = jnp.dot(
        named.astype(jnp.bfloat16),
        before.astype(jnp.float32).astype(jnp.bfloat16),
        preferred_element_type=jnp.float32,
    )
    slot = jnp.sum(earlier * named, axis=0, keepdims=True).astype(jnp.int32)
    code = dest * capacity + slot
    chosen = lax.broadcasted_iota(jnp.int32, (slots, rows), 0) == code
    chosen_f = chosen.astype(jnp.float32)
    moved = jnp.dot(
        chosen_f.astype(jnp.bfloat16), rows_ref[...], preferred_element_type=jnp.float32
    )
    out_ref[:, :, :width] = moved.astype(jnp.bfloat16).reshape(owners, capacity, width)
    bands = jnp.sum(
        chosen_f * (band_ref[...] + BAND_SHIFT).astype(jnp.float32), axis=1, keepdims=True
    )
    out_ref[:, :, width:] = (
        jnp.broadcast_to(bands, (slots, BAND_LANES))
        .astype(jnp.bfloat16)
        .reshape(owners, capacity, BAND_LANES)
    )


def pack(audio_rows, destination, row_band, owners, capacity):
    rows, width = audio_rows.shape

    def body(*refs):
        pack_kernel(owners, capacity, *refs)

    return pl.pallas_call(
        body,
        out_shape=jax.ShapeDtypeStruct((owners, capacity, width + BAND_LANES), jnp.bfloat16),
        name="pack",
    )(destination.reshape(1, rows), row_band.reshape(1, rows), audio_rows)


def attend_kernel(
    band_ref, slots_ref, latents_ref, query_ref, wk_ref, wv_ref, nk_ref, nv_ref, wo_ref, out_ref, acc_ref
):
    step = pl.program_id(0)
    width = latents_ref.shape[1]
    slots = slots_ref.shape[0] * slots_ref.shape[1]
    scale = 1.0 / float(HD) ** 0.5

    @pl.when(step == 0)
    def _():
        acc_ref[...] = latents_ref[...].astype(jnp.float32)

    frames = slots_ref[:, :, :width].reshape(slots, width)
    bands = slots_ref[:, :, width:].reshape(slots, BAND_LANES).astype(jnp.float32)
    here = (band_ref[0] + BAND_SHIFT).astype(jnp.float32)
    usable = jnp.abs(jnp.transpose(bands) - here) <= 1.0
    keys = jnp.dot(frames, wk_ref[...], preferred_element_type=jnp.float32).astype(jnp.bfloat16)
    values = jnp.dot(frames, wv_ref[...], preferred_element_type=jnp.float32).astype(jnp.bfloat16)
    attended = []
    for h in range(wk_ref.shape[1] // HD):
        cols = slice(h * HD, (h + 1) * HD)
        query = query_ref[:, cols]
        score = (
            lax.dot_general(
                query, keys[:, cols], (((1,), (1,)), ((), ())), preferred_element_type=jnp.float32
            )
            * scale
        )
        null = (
            jnp.sum(query.astype(jnp.float32) * nk_ref[:, cols], axis=1, keepdims=True) * scale
        )
        masked = jnp.where(usable, score, -1e30)
        highest = jnp.maximum(jnp.max(masked, axis=1, keepdims=True), null)
        expo = jnp.where(usable, jnp.exp(masked - highest), 0.0)
        null_expo = jnp.exp(null - highest)
        total = jnp.sum(expo, axis=1, keepdims=True) + null_expo
        inverse = 1.0 / total
        weights = (expo * inverse).astype(jnp.bfloat16)
        null_weight = (null_expo * inverse).astype(jnp.bfloat16).astype(jnp.float32)
        summed = jnp.dot(weights, values[:, cols], preferred_element_type=jnp.float32)
        attended.append((summed + null_weight * nv_ref[:, cols]).astype(jnp.bfloat16))
    acc_ref[...] += jnp.dot(
        jnp.concatenate(attended, axis=1), wo_ref[...], preferred_element_type=jnp.float32
    )

    @pl.when(step == pl.num_programs(0) - 1)
    def _():
        out_ref[...] = acc_ref[...].astype(jnp.bfloat16)


def attend(slots, block_band, latents, wk, wv, null_key, null_value, out_weight):
    count, width = latents.shape
    step = 2 * HD
    return pl.pallas_call(
        attend_kernel,
        grid=(width // step,),
        in_specs=[
            pl.BlockSpec(memory_space=pltpu.SMEM),
            pl.BlockSpec(slots.shape, lambda i: (0, 0, 0)),
            pl.BlockSpec((count, width), lambda i: (0, 0)),
            pl.BlockSpec((count, step), lambda i: (0, i)),
            pl.BlockSpec((width, step), lambda i: (0, i)),
            pl.BlockSpec((width, step), lambda i: (0, i)),
            pl.BlockSpec((1, step), lambda i: (0, i)),
            pl.BlockSpec((1, step), lambda i: (0, i)),
            pl.BlockSpec((step, width), lambda i: (i, 0)),
        ],
        out_specs=pl.BlockSpec((count, width), lambda i: (0, 0)),
        out_shape=jax.ShapeDtypeStruct((count, width), jnp.bfloat16),
        scratch_shapes=[pltpu.VMEM((count, width), jnp.float32)],
        name="attend",
    )(
        block_band,
        slots,
        latents,
        latents,
        wk,
        wv,
        null_key.reshape(1, width),
        null_value.reshape(1, width),
        out_weight,
    )


def local(
    audio_rows,
    routing,
    row_band,
    block_band,
    latents,
    kv_weight,
    null_key,
    null_value,
    out_weight,
    mlp_gain,
    up_weight,
    down_weight,
):
    local_rows = audio_rows.shape[0]
    width = latents.shape[1]
    owners = lax.axis_size("tm")
    groups = lax.axis_size("grp")
    capacity = max(2, 2 * local_rows // owners)

    payload = pack(audio_rows, routing[:, 0], row_band, owners, capacity)
    slots = lax.all_to_all(payload, "tm", split_axis=0, concat_axis=0, tiled=True)

    shard = jnp.concatenate(
        [kv_weight[:, :width], kv_weight[:, width:], up_weight, jnp.transpose(down_weight)], axis=0
    )
    shard = (shard.astype(jnp.float32) * WEIGHT_SCALE).astype(jnp.float16)
    gathered = lax.all_gather(shard, "tm", axis=0, tiled=True)
    gathered = gathered.reshape(owners, 4, kv_weight.shape[0], width)

    def whole(index):
        part = gathered[:, index].astype(jnp.float32) * (1.0 / WEIGHT_SCALE)
        return part.astype(jnp.bfloat16).reshape(width, width)

    joined = attend(
        slots, block_band, latents, whole(0), whole(1), null_key, null_value, out_weight
    )
    sent = (joined.astype(jnp.float32) * JOINED_SCALE).astype(jnp.float16)
    window = lax.all_gather(sent, "grp", axis=0, tiled=True)
    values = window.astype(jnp.float32) * (1.0 / JOINED_SCALE)
    center = values - jnp.mean(values, axis=-1, keepdims=True)
    spread = jnp.mean(center * center, axis=-1, keepdims=True)
    normed = (center * lax.rsqrt(spread + 1e-05) * mlp_gain).astype(jnp.bfloat16)
    hidden = jax.nn.gelu(jnp.dot(normed, whole(2), preferred_element_type=jnp.float32)).astype(
        jnp.bfloat16
    )
    down_rows = whole(3)
    me = lax.axis_index("grp")
    columns = width // groups

    def term(offset):
        owner = lax.rem(me + offset + groups, groups)
        rows = lax.dynamic_slice_in_dim(down_rows, owner * columns, columns, 0)
        return lax.dot_general(
            hidden, rows, (((1,), (1,)), ((), ())), preferred_element_type=jnp.float32
        )

    def hop(values, by):
        pairs = [(i, (i + by) % groups) for i in range(groups)]
        return lax.ppermute(values.astype(jnp.bfloat16), "grp", pairs)

    up_hops = groups // 2
    down_hops = groups - 1 - up_hops
    rising = hop(term(up_hops), 1)
    falling = hop(term(-down_hops), -1)
    for distance in range(1, up_hops):
        rising = hop(rising.astype(jnp.float32) + term(up_hops - distance), 1)
        if distance < down_hops:
            falling = hop(falling.astype(jnp.float32) + term(distance - down_hops), -1)
    residual = lax.dynamic_slice_in_dim(window, me * columns, columns, 1)
    total = term(0) + rising.astype(jnp.float32) + falling.astype(jnp.float32)
    return (residual.astype(jnp.float32) * (1.0 / JOINED_SCALE) + total).astype(jnp.bfloat16)


def solution(mesh):
    return jax.shard_map(
        local,
        mesh=mesh,
        in_specs=(
            P(("grp", "tm"), None),
            P(("grp", "tm"), None),
            P(("grp", "tm")),
            P(("grp", "tm")),
            P(("grp", "tm"), None),
            P("tm", None),
            P(),
            P(),
            P(),
            P(),
            P("tm", "grp"),
            P("grp", "tm"),
        ),
        out_specs=P("tm", "grp"),
        check_vma=False,
    )
```

```python
import jax
import jax.numpy as jnp
from jax import lax
from jax.experimental import pallas as pl
from jax.experimental.pallas import tpu as pltpu
from jax.sharding import PartitionSpec as P


HD = 128
BAND_LANES = 128
BAND_SHIFT = 4
WEIGHT_SCALE = 2.0**17
JOINED_SCALE = 0.25


def pack_kernel(owners, capacity, dest_ref, band_ref, rows_ref, out_ref):
    rows = rows_ref.shape[0]
    width = rows_ref.shape[1]
    slots = owners * capacity
    dest = dest_ref[...]
    owner_ids = lax.broadcasted_iota(jnp.int32, (owners, rows), 0)
    named = (owner_ids == dest).astype(jnp.float32)
    before = lax.broadcasted_iota(jnp.int32, (rows, rows), 0) < lax.broadcasted_iota(
        jnp.int32, (rows, rows), 1
    )
    earlier = jnp.dot(
        named.astype(jnp.bfloat16),
        before.astype(jnp.float32).astype(jnp.bfloat16),
        preferred_element_type=jnp.float32,
    )
    slot = jnp.sum(earlier * named, axis=0, keepdims=True).astype(jnp.int32)
    code = dest * capacity + slot
    chosen = lax.broadcasted_iota(jnp.int32, (slots, rows), 0) == code
    chosen_f = chosen.astype(jnp.float32)
    moved = jnp.dot(
        chosen_f.astype(jnp.bfloat16), rows_ref[...], preferred_element_type=jnp.float32
    )
    out_ref[:, :, :width] = moved.astype(jnp.bfloat16).reshape(owners, capacity, width)
    bands = jnp.sum(
        chosen_f * (band_ref[...] + BAND_SHIFT).astype(jnp.float32), axis=1, keepdims=True
    )
    out_ref[:, :, width:] = (
        jnp.broadcast_to(bands, (slots, BAND_LANES))
        .astype(jnp.bfloat16)
        .reshape(owners, capacity, BAND_LANES)
    )


def pack(audio_rows, destination, row_band, owners, capacity):
    rows, width = audio_rows.shape

    def body(*refs):
        pack_kernel(owners, capacity, *refs)

    return pl.pallas_call(
        body,
        out_shape=jax.ShapeDtypeStruct((owners, capacity, width + BAND_LANES), jnp.bfloat16),
        name="pack",
    )(destination.reshape(1, rows), row_band.reshape(1, rows), audio_rows)


def attend_kernel(
    band_ref,
    slots_ref,
    latents_ref,
    query_ref,
    wk_ref,
    wv_ref,
    nk_ref,
    nv_ref,
    wo_ref,
    out_ref,
    acc_ref,
    away_ref,
):
    step = pl.program_id(0)
    width = latents_ref.shape[1]
    slots = slots_ref.shape[0] * slots_ref.shape[1]
    scale = 1.0 / float(HD) ** 0.5

    @pl.when(step == 0)
    def _():
        acc_ref[...] = latents_ref[...].astype(jnp.float32)
        bands = slots_ref[:, :, width:].reshape(slots, BAND_LANES).astype(jnp.float32)
        here = (band_ref[0] + BAND_SHIFT).astype(jnp.float32)
        away_ref[...] = jnp.abs(jnp.transpose(bands) - here)

    frames = slots_ref[:, :, :width].reshape(slots, width)
    usable = away_ref[...] <= 1.0
    keys = jnp.dot(frames, wk_ref[...], preferred_element_type=jnp.float32).astype(jnp.bfloat16)
    values = jnp.dot(frames, wv_ref[...], preferred_element_type=jnp.float32).astype(jnp.bfloat16)
    attended = []
    for h in range(wk_ref.shape[1] // HD):
        cols = slice(h * HD, (h + 1) * HD)
        query = query_ref[:, cols]
        score = (
            lax.dot_general(
                query, keys[:, cols], (((1,), (1,)), ((), ())), preferred_element_type=jnp.float32
            )
            * scale
        )
        null = (
            jnp.sum(query.astype(jnp.float32) * nk_ref[:, cols], axis=1, keepdims=True) * scale
        )
        masked = jnp.where(usable, score, -1e30)
        highest = jnp.maximum(jnp.max(masked, axis=1, keepdims=True), null)
        expo = jnp.where(usable, jnp.exp(masked - highest), 0.0)
        null_expo = jnp.exp(null - highest)
        total = jnp.sum(expo, axis=1, keepdims=True) + null_expo
        inverse = 1.0 / total
        weights = (expo * inverse).astype(jnp.bfloat16)
        null_weight = (null_expo * inverse).astype(jnp.bfloat16).astype(jnp.float32)
        summed = jnp.dot(weights, values[:, cols], preferred_element_type=jnp.float32)
        attended.append((summed + null_weight * nv_ref[:, cols]).astype(jnp.bfloat16))
    acc_ref[...] += jnp.dot(
        jnp.concatenate(attended, axis=1), wo_ref[...], preferred_element_type=jnp.float32
    )

    @pl.when(step == pl.num_programs(0) - 1)
    def _():
        out_ref[...] = acc_ref[...].astype(jnp.bfloat16)


def attend(slots, block_band, latents, wk, wv, null_key, null_value, out_weight):
    count, width = latents.shape
    step = 4 * HD
    return pl.pallas_call(
        attend_kernel,
        grid=(width // step,),
        in_specs=[
            pl.BlockSpec(memory_space=pltpu.SMEM),
            pl.BlockSpec(slots.shape, lambda i: (0, 0, 0)),
            pl.BlockSpec((count, width), lambda i: (0, 0)),
            pl.BlockSpec((count, step), lambda i: (0, i)),
            pl.BlockSpec((width, step), lambda i: (0, i)),
            pl.BlockSpec((width, step), lambda i: (0, i)),
            pl.BlockSpec((1, step), lambda i: (0, i)),
            pl.BlockSpec((1, step), lambda i: (0, i)),
            pl.BlockSpec((step, width), lambda i: (i, 0)),
        ],
        out_specs=pl.BlockSpec((count, width), lambda i: (0, 0)),
        out_shape=jax.ShapeDtypeStruct((count, width), jnp.bfloat16),
        scratch_shapes=[
            pltpu.VMEM((count, width), jnp.float32),
            pltpu.VMEM((count, slots.shape[0] * slots.shape[1]), jnp.float32),
        ],
        name="attend",
    )(
        block_band,
        slots,
        latents,
        latents,
        wk,
        wv,
        null_key.reshape(1, width),
        null_value.reshape(1, width),
        out_weight,
    )


def local(
    audio_rows,
    routing,
    row_band,
    block_band,
    latents,
    kv_weight,
    null_key,
    null_value,
    out_weight,
    mlp_gain,
    up_weight,
    down_weight,
):
    local_rows = audio_rows.shape[0]
    width = latents.shape[1]
    owners = lax.axis_size("tm")
    groups = lax.axis_size("grp")
    capacity = max(2, 2 * local_rows // owners)

    payload = pack(audio_rows, routing[:, 0], row_band, owners, capacity)
    slots = lax.all_to_all(payload, "tm", split_axis=0, concat_axis=0, tiled=True)

    shard = jnp.concatenate(
        [kv_weight[:, :width], kv_weight[:, width:], up_weight, jnp.transpose(down_weight)], axis=0
    )
    shard = (shard.astype(jnp.float32) * WEIGHT_SCALE).astype(jnp.float16)
    gathered = lax.all_gather(shard, "tm", axis=0, tiled=True)
    gathered = gathered.reshape(owners, 4, kv_weight.shape[0], width)

    def whole(index):
        part = gathered[:, index].astype(jnp.float32) * (1.0 / WEIGHT_SCALE)
        return part.astype(jnp.bfloat16).reshape(width, width)

    joined = attend(
        slots, block_band, latents, whole(0), whole(1), null_key, null_value, out_weight
    )
    sent = (joined.astype(jnp.float32) * JOINED_SCALE).astype(jnp.float16)
    window = lax.all_gather(sent, "grp", axis=0, tiled=True)
    values = window.astype(jnp.float32) * (1.0 / JOINED_SCALE)
    center = values - jnp.mean(values, axis=-1, keepdims=True)
    spread = jnp.mean(center * center, axis=-1, keepdims=True)
    normed = (center * lax.rsqrt(spread + 1e-05) * mlp_gain).astype(jnp.bfloat16)
    hidden = jax.nn.gelu(jnp.dot(normed, whole(2), preferred_element_type=jnp.float32)).astype(
        jnp.bfloat16
    )
    down_rows = whole(3)
    me = lax.axis_index("grp")
    columns = width // groups

    def term(offset):
        owner = lax.rem(me + offset + groups, groups)
        rows = lax.dynamic_slice_in_dim(down_rows, owner * columns, columns, 0)
        return lax.optimization_barrier(
            lax.dot_general(
                hidden, rows, (((1,), (1,)), ((), ())), preferred_element_type=jnp.float32
            )
        )

    def hop(values, by):
        pairs = [(i, (i + by) % groups) for i in range(groups)]
        values = values.astype(jnp.bfloat16)
        return lax.ppermute(values, "grp", pairs)

    up_hops = groups // 2
    down_hops = groups - 1 - up_hops
    rising = hop(term(up_hops), 1)
    falling = hop(term(-down_hops), -1)
    for distance in range(1, up_hops):
        rising = hop(rising.astype(jnp.float32) + term(up_hops - distance), 1)
        if distance < down_hops:
            falling = hop(falling.astype(jnp.float32) + term(distance - down_hops), -1)
    residual = lax.dynamic_slice_in_dim(window, me * columns, columns, 1)
    total = term(0) + rising.astype(jnp.float32) + falling.astype(jnp.float32)
    return (residual.astype(jnp.float32) * (1.0 / JOINED_SCALE) + total).astype(jnp.bfloat16)


def solution(mesh):
    return jax.shard_map(
        local,
        mesh=mesh,
        in_specs=(
            P(("grp", "tm"), None),
            P(("grp", "tm"), None),
            P(("grp", "tm")),
            P(("grp", "tm")),
            P(("grp", "tm"), None),
            P("tm", None),
            P(),
            P(),
            P(),
            P(),
            P("tm", "grp"),
            P("grp", "tm"),
        ),
        out_specs=P("tm", "grp"),
        check_vma=False,
    )
```

```python
import jax
import jax.numpy as jnp
from jax import lax
from jax.experimental import pallas as pl
from jax.experimental.pallas import tpu as pltpu
from jax.sharding import PartitionSpec as P


HD = 128
BAND_LANES = 128
FEATURES = 128
LINES = 8
BAND_SHIFT = 4
WEIGHT_SCALE = 2.0**17
JOINED_SCALE = 0.25


def pack_kernel(owners, capacity, dest_ref, band_ref, rows_ref, out_ref):
    rows = rows_ref.shape[0]
    width = rows_ref.shape[1]
    slots = owners * capacity
    dest = dest_ref[...]
    owner_ids = lax.broadcasted_iota(jnp.int32, (owners, rows), 0)
    named = (owner_ids == dest).astype(jnp.float32)
    before = lax.broadcasted_iota(jnp.int32, (rows, rows), 0) < lax.broadcasted_iota(
        jnp.int32, (rows, rows), 1
    )
    earlier = jnp.dot(
        named.astype(jnp.bfloat16),
        before.astype(jnp.float32).astype(jnp.bfloat16),
        preferred_element_type=jnp.float32,
    )
    slot = jnp.sum(earlier * named, axis=0, keepdims=True).astype(jnp.int32)
    code = dest * capacity + slot
    chosen = lax.broadcasted_iota(jnp.int32, (slots, rows), 0) == code
    chosen_f = chosen.astype(jnp.float32)
    moved = jnp.dot(
        chosen_f.astype(jnp.bfloat16), rows_ref[...], preferred_element_type=jnp.float32
    )
    out_ref[:, :, :width] = moved.astype(jnp.bfloat16).reshape(owners, capacity, width)
    bands = jnp.sum(
        chosen_f * (band_ref[...] + BAND_SHIFT).astype(jnp.float32), axis=1, keepdims=True
    )
    out_ref[:, :, width:] = (
        jnp.broadcast_to(bands, (slots, BAND_LANES))
        .astype(jnp.bfloat16)
        .reshape(owners, capacity, BAND_LANES)
    )


def pack(audio_rows, destination, row_band, owners, capacity):
    rows, width = audio_rows.shape

    def body(*refs):
        pack_kernel(owners, capacity, *refs)

    return pl.pallas_call(
        body,
        out_shape=jax.ShapeDtypeStruct((owners, capacity, width + BAND_LANES), jnp.bfloat16),
        name="pack",
    )(destination.reshape(1, rows), row_band.reshape(1, rows), audio_rows)


def attend_kernel(
    band_ref,
    slots_ref,
    latents_ref,
    query_ref,
    wk_ref,
    wv_ref,
    nk_ref,
    nv_ref,
    wo_ref,
    out_ref,
    acc_ref,
    away_ref,
    frames_ref,
):
    step = pl.program_id(0)
    width = latents_ref.shape[1]
    slots = slots_ref.shape[0] * slots_ref.shape[1]
    scale = 1.0 / float(HD) ** 0.5

    @pl.when(step == 0)
    def _():
        acc_ref[...] = latents_ref[...].astype(jnp.float32)
        bands = slots_ref[:, :, width:].reshape(slots, BAND_LANES).astype(jnp.float32)
        here = (band_ref[0] + BAND_SHIFT).astype(jnp.float32)
        away_ref[...] = jnp.abs(jnp.transpose(bands) - here)
        parts = width // FEATURES
        own = lax.axis_index("tm") // (lax.axis_size("tm") // parts)
        for part in range(parts):
            start = pl.multiple_of(lax.rem(own + part, parts) * FEATURES, FEATURES)
            frames_ref[:, part * FEATURES : (part + 1) * FEATURES] = slots_ref[
                :, :, pl.ds(start, FEATURES)
            ].reshape(slots, FEATURES)

    frames = frames_ref[...]
    usable = away_ref[...] <= 1.0
    keys = jnp.dot(frames, wk_ref[...], preferred_element_type=jnp.float32).astype(jnp.bfloat16)
    values = jnp.dot(frames, wv_ref[...], preferred_element_type=jnp.float32).astype(jnp.bfloat16)
    attended = []
    for h in range(wk_ref.shape[1] // HD):
        cols = slice(h * HD, (h + 1) * HD)
        query = query_ref[:, cols]
        score = (
            lax.dot_general(
                query, keys[:, cols], (((1,), (1,)), ((), ())), preferred_element_type=jnp.float32
            )
            * scale
        )
        null = (
            jnp.sum(query.astype(jnp.float32) * nk_ref[:, cols], axis=1, keepdims=True) * scale
        )
        masked = jnp.where(usable, score, -1e30)
        highest = jnp.maximum(jnp.max(masked, axis=1, keepdims=True), null)
        expo = jnp.where(usable, jnp.exp(masked - highest), 0.0)
        null_expo = jnp.exp(null - highest)
        total = jnp.sum(expo, axis=1, keepdims=True) + null_expo
        inverse = 1.0 / total
        weights = (expo * inverse).astype(jnp.bfloat16)
        null_weight = (null_expo * inverse).astype(jnp.bfloat16).astype(jnp.float32)
        summed = jnp.dot(weights, values[:, cols], preferred_element_type=jnp.float32)
        attended.append((summed + null_weight * nv_ref[:, cols]).astype(jnp.bfloat16))
    acc_ref[...] += jnp.dot(
        jnp.concatenate(attended, axis=1), wo_ref[...], preferred_element_type=jnp.float32
    )

    @pl.when(step == pl.num_programs(0) - 1)
    def _():
        out_ref[...] = acc_ref[...].astype(jnp.bfloat16)


def attend(slots, block_band, latents, wk, wv, null_key, null_value, out_weight):
    count, width = latents.shape
    step = 4 * HD
    return pl.pallas_call(
        attend_kernel,
        grid=(width // step,),
        in_specs=[
            pl.BlockSpec(memory_space=pltpu.SMEM),
            pl.BlockSpec(slots.shape, lambda i: (0, 0, 0)),
            pl.BlockSpec((count, width), lambda i: (0, 0)),
            pl.BlockSpec((count, step), lambda i: (0, i)),
            pl.BlockSpec((width, step), lambda i: (0, i)),
            pl.BlockSpec((width, step), lambda i: (0, i)),
            pl.BlockSpec((1, step), lambda i: (0, i)),
            pl.BlockSpec((1, step), lambda i: (0, i)),
            pl.BlockSpec((step, width), lambda i: (i, 0)),
        ],
        out_specs=pl.BlockSpec((count, width), lambda i: (0, 0)),
        out_shape=jax.ShapeDtypeStruct((count, width), jnp.bfloat16),
        scratch_shapes=[
            pltpu.VMEM((count, width), jnp.float32),
            pltpu.VMEM((count, slots.shape[0] * slots.shape[1]), jnp.float32),
            pltpu.VMEM((slots.shape[0] * slots.shape[1], width), jnp.bfloat16),
        ],
        name="attend",
    )(
        block_band,
        slots,
        latents,
        latents,
        wk,
        wv,
        null_key.reshape(1, width),
        null_value.reshape(1, width),
        out_weight,
    )


def local(
    audio_rows,
    routing,
    row_band,
    block_band,
    latents,
    kv_weight,
    null_key,
    null_value,
    out_weight,
    mlp_gain,
    up_weight,
    down_weight,
):
    local_rows = audio_rows.shape[0]
    width = latents.shape[1]
    owners = lax.axis_size("tm")
    groups = lax.axis_size("grp")
    capacity = max(2, 2 * local_rows // owners)

    line = owners // LINES
    half = groups // 2

    late = lax.all_gather(
        jnp.concatenate([up_weight, jnp.transpose(down_weight)], axis=0), "tm", axis=0, tiled=True
    ).reshape(owners, 2, up_weight.shape[0], width)
    up_rows = late[:, 0].reshape(width, width)
    down_rows = late[:, 1].reshape(width, width)

    shard = jnp.concatenate([kv_weight[:, :width], kv_weight[:, width:]], axis=0)
    shard = (shard.astype(jnp.float32) * WEIGHT_SCALE).astype(jnp.float16)
    fetched = []
    for j in range(LINES // half):
        pairs = []
        for g in range(groups):
            for source in range(LINES):
                target = (source - (LINES // half) * (g % half) - j) % LINES
                for k in range(line):
                    pairs.append(
                        (
                            g * owners + source * line + k,
                            g * owners + target * line + k,
                        )
                    )
        fetched.append(lax.ppermute(shard, ("grp", "tm"), pairs))

    payload = pack(audio_rows, routing[:, 0], row_band, owners, capacity)
    payload, fetched = lax.optimization_barrier((payload, jnp.concatenate(fetched, axis=0)))
    slots = lax.all_to_all(payload, "tm", split_axis=0, concat_axis=0, tiled=True)
    lines = lax.all_gather(
        fetched,
        "grp",
        axis=0,
        tiled=True,
        axis_index_groups=[list(range(h * half, (h + 1) * half)) for h in range(2)],
    )
    gathered = lax.all_gather(
        lines,
        "tm",
        axis=0,
        tiled=True,
        axis_index_groups=[list(range(z * line, (z + 1) * line)) for z in range(LINES)],
    ).reshape(line, LINES, 2, kv_weight.shape[0], width)

    def whole(index):
        part = jnp.transpose(gathered[:, :, index], (1, 0, 2, 3)).astype(jnp.float32)
        return (part * (1.0 / WEIGHT_SCALE)).astype(jnp.bfloat16).reshape(width, width)

    joined = attend(
        slots, block_band, latents, whole(0), whole(1), null_key, null_value, out_weight
    )
    sent = (joined.astype(jnp.float32) * JOINED_SCALE).astype(jnp.float16)
    window = lax.all_gather(sent, "grp", axis=0, tiled=True)
    values = window.astype(jnp.float32) * (1.0 / JOINED_SCALE)
    center = values - jnp.mean(values, axis=-1, keepdims=True)
    spread = jnp.mean(center * center, axis=-1, keepdims=True)
    normed = (center * lax.rsqrt(spread + 1e-05) * mlp_gain).astype(jnp.bfloat16)
    hidden = jax.nn.gelu(jnp.dot(normed, up_rows, preferred_element_type=jnp.float32)).astype(
        jnp.bfloat16
    )
    me = lax.axis_index("grp")
    columns = width // groups

    def term(offset):
        owner = lax.rem(me + offset + groups, groups)
        rows = lax.dynamic_slice_in_dim(down_rows, owner * columns, columns, 0)
        return lax.optimization_barrier(
            lax.dot_general(
                hidden, rows, (((1,), (1,)), ((), ())), preferred_element_type=jnp.float32
            )
        )

    def hop(values, by):
        pairs = [(i, (i + by) % groups) for i in range(groups)]
        values = values.astype(jnp.bfloat16)
        return lax.ppermute(values, "grp", pairs)

    up_hops = groups // 2
    down_hops = groups - 1 - up_hops
    rising = hop(term(up_hops), 1)
    falling = hop(term(-down_hops), -1)
    for distance in range(1, up_hops):
        rising = hop(rising.astype(jnp.float32) + term(up_hops - distance), 1)
        if distance < down_hops:
            falling = hop(falling.astype(jnp.float32) + term(distance - down_hops), -1)
    residual = lax.dynamic_slice_in_dim(window, me * columns, columns, 1)
    total = term(0) + rising.astype(jnp.float32) + falling.astype(jnp.float32)
    return (residual.astype(jnp.float32) * (1.0 / JOINED_SCALE) + total).astype(jnp.bfloat16)


def solution(mesh):
    return jax.shard_map(
        local,
        mesh=mesh,
        in_specs=(
            P(("grp", "tm"), None),
            P(("grp", "tm"), None),
            P(("grp", "tm")),
            P(("grp", "tm")),
            P(("grp", "tm"), None),
            P("tm", None),
            P(),
            P(),
            P(),
            P(),
            P("tm", "grp"),
            P("grp", "tm"),
        ),
        out_specs=P("tm", "grp"),
        check_vma=False,
    )
```

```python
import jax
import jax.numpy as jnp
from jax import lax
from jax.experimental import pallas as pl
from jax.experimental.pallas import tpu as pltpu
from jax.sharding import PartitionSpec as P


HD = 128
BAND_LANES = 128
FEATURES = 128
LINES = 8
BAND_SHIFT = 4
WEIGHT_SCALE = 2.0**17
JOINED_SCALE = 0.25


def pack_kernel(owners, capacity, dest_ref, band_ref, rows_ref, out_ref):
    rows = rows_ref.shape[0]
    width = rows_ref.shape[1]
    slots = owners * capacity
    dest = dest_ref[...]
    owner_ids = lax.broadcasted_iota(jnp.int32, (owners, rows), 0)
    named = (owner_ids == dest).astype(jnp.float32)
    before = lax.broadcasted_iota(jnp.int32, (rows, rows), 0) < lax.broadcasted_iota(
        jnp.int32, (rows, rows), 1
    )
    earlier = jnp.dot(
        named.astype(jnp.bfloat16),
        before.astype(jnp.float32).astype(jnp.bfloat16),
        preferred_element_type=jnp.float32,
    )
    slot = jnp.sum(earlier * named, axis=0, keepdims=True).astype(jnp.int32)
    code = dest * capacity + slot
    chosen = lax.broadcasted_iota(jnp.int32, (slots, rows), 0) == code
    chosen_f = chosen.astype(jnp.float32)
    moved = jnp.dot(
        chosen_f.astype(jnp.bfloat16), rows_ref[...], preferred_element_type=jnp.float32
    )
    out_ref[:, :, :width] = moved.astype(jnp.bfloat16).reshape(owners, capacity, width)
    bands = jnp.sum(
        chosen_f * (band_ref[...] + BAND_SHIFT).astype(jnp.float32), axis=1, keepdims=True
    )
    out_ref[:, :, width:] = (
        jnp.broadcast_to(bands, (slots, BAND_LANES))
        .astype(jnp.bfloat16)
        .reshape(owners, capacity, BAND_LANES)
    )


def pack(audio_rows, destination, row_band, owners, capacity):
    rows, width = audio_rows.shape

    def body(*refs):
        pack_kernel(owners, capacity, *refs)

    return pl.pallas_call(
        body,
        out_shape=jax.ShapeDtypeStruct((owners, capacity, width + BAND_LANES), jnp.bfloat16),
        name="pack",
    )(destination.reshape(1, rows), row_band.reshape(1, rows), audio_rows)


def attend_kernel(
    band_ref,
    slots_ref,
    latents_ref,
    query_ref,
    wk_ref,
    wv_ref,
    nk_ref,
    nv_ref,
    wo_ref,
    out_ref,
    acc_ref,
    away_ref,
    frames_ref,
):
    step = pl.program_id(0)
    width = latents_ref.shape[1]
    slots = slots_ref.shape[0] * slots_ref.shape[1]
    scale = 1.0 / float(HD) ** 0.5

    @pl.when(step == 0)
    def _():
        acc_ref[...] = latents_ref[...].astype(jnp.float32)
        bands = slots_ref[:, :, width:].reshape(slots, BAND_LANES).astype(jnp.float32)
        here = (band_ref[0] + BAND_SHIFT).astype(jnp.float32)
        away_ref[...] = jnp.abs(jnp.transpose(bands) - here)
        parts = width // FEATURES
        own = lax.axis_index("tm") // (lax.axis_size("tm") // parts)
        for part in range(parts):
            start = pl.multiple_of(lax.rem(own + part, parts) * FEATURES, FEATURES)
            frames_ref[:, part * FEATURES : (part + 1) * FEATURES] = slots_ref[
                :, :, pl.ds(start, FEATURES)
            ].reshape(slots, FEATURES)

    frames = frames_ref[...]
    usable = away_ref[...] <= 1.0

    def rows_of(ref):
        return jnp.concatenate(
            [ref[:, part].reshape(FEATURES, ref.shape[3]) for part in range(ref.shape[1])], axis=0
        )

    keys = jnp.dot(frames, rows_of(wk_ref), preferred_element_type=jnp.float32).astype(jnp.bfloat16)
    values = jnp.dot(frames, rows_of(wv_ref), preferred_element_type=jnp.float32).astype(jnp.bfloat16)
    attended = []
    for h in range(wk_ref.shape[3] // HD):
        cols = slice(h * HD, (h + 1) * HD)
        query = query_ref[:, cols]
        score = (
            lax.dot_general(
                query, keys[:, cols], (((1,), (1,)), ((), ())), preferred_element_type=jnp.float32
            )
            * scale
        )
        null = (
            jnp.sum(query.astype(jnp.float32) * nk_ref[:, cols], axis=1, keepdims=True) * scale
        )
        masked = jnp.where(usable, score, -1e30)
        highest = jnp.maximum(jnp.max(masked, axis=1, keepdims=True), null)
        expo = jnp.where(usable, jnp.exp(masked - highest), 0.0)
        null_expo = jnp.exp(null - highest)
        total = jnp.sum(expo, axis=1, keepdims=True) + null_expo
        inverse = 1.0 / total
        weights = (expo * inverse).astype(jnp.bfloat16)
        null_weight = (null_expo * inverse).astype(jnp.bfloat16).astype(jnp.float32)
        summed = jnp.dot(weights, values[:, cols], preferred_element_type=jnp.float32)
        attended.append((summed + null_weight * nv_ref[:, cols]).astype(jnp.bfloat16))
    acc_ref[...] += jnp.dot(
        jnp.concatenate(attended, axis=1), wo_ref[...], preferred_element_type=jnp.float32
    )

    @pl.when(step == pl.num_programs(0) - 1)
    def _():
        out_ref[...] = acc_ref[...].astype(jnp.bfloat16)


def attend(slots, block_band, latents, kv, null_key, null_value, out_weight):
    count, width = latents.shape
    step = 4 * HD
    return pl.pallas_call(
        attend_kernel,
        grid=(width // step,),
        in_specs=[
            pl.BlockSpec(memory_space=pltpu.SMEM),
            pl.BlockSpec(slots.shape, lambda i: (0, 0, 0)),
            pl.BlockSpec((count, width), lambda i: (0, 0)),
            pl.BlockSpec((count, step), lambda i: (0, i)),
            pl.BlockSpec((*kv.shape[:2], None, kv.shape[3], step), lambda i: (0, 0, 0, 0, i)),
            pl.BlockSpec((*kv.shape[:2], None, kv.shape[3], step), lambda i: (0, 0, 1, 0, i)),
            pl.BlockSpec((1, step), lambda i: (0, i)),
            pl.BlockSpec((1, step), lambda i: (0, i)),
            pl.BlockSpec((step, width), lambda i: (i, 0)),
        ],
        out_specs=pl.BlockSpec((count, width), lambda i: (0, 0)),
        out_shape=jax.ShapeDtypeStruct((count, width), jnp.bfloat16),
        scratch_shapes=[
            pltpu.VMEM((count, width), jnp.float32),
            pltpu.VMEM((count, slots.shape[0] * slots.shape[1]), jnp.float32),
            pltpu.VMEM((slots.shape[0] * slots.shape[1], width), jnp.bfloat16),
        ],
        name="attend",
    )(
        block_band,
        slots,
        latents,
        latents,
        kv,
        kv,
        null_key.reshape(1, width),
        null_value.reshape(1, width),
        out_weight,
    )


def local(
    audio_rows,
    routing,
    row_band,
    block_band,
    latents,
    kv_weight,
    null_key,
    null_value,
    out_weight,
    mlp_gain,
    up_weight,
    down_weight,
):
    local_rows = audio_rows.shape[0]
    width = latents.shape[1]
    owners = lax.axis_size("tm")
    groups = lax.axis_size("grp")
    capacity = max(2, 2 * local_rows // owners)

    line = owners // LINES

    late = lax.all_gather(
        jnp.concatenate([up_weight, jnp.transpose(down_weight)], axis=0), "tm", axis=0, tiled=True
    ).reshape(owners, 2, up_weight.shape[0], width)
    up_rows = late[:, 0].reshape(width, width)
    down_rows = late[:, 1].reshape(width, width)

    shard = jnp.concatenate([kv_weight[:, :width], kv_weight[:, width:]], axis=0)
    shard = (shard.astype(jnp.float32) * WEIGHT_SCALE).astype(jnp.float16)
    fetched = [shard]
    for shift in range(1, LINES):
        pairs = [(i, (i - shift * line) % owners) for i in range(owners)]
        fetched.append(lax.ppermute(shard, "tm", pairs))

    payload = pack(audio_rows, routing[:, 0], row_band, owners, capacity)
    slots = lax.all_to_all(payload, "tm", split_axis=0, concat_axis=0, tiled=True)
    gathered = lax.all_gather(
        jnp.concatenate(fetched, axis=0),
        "tm",
        axis=0,
        tiled=True,
        axis_index_groups=[list(range(z * line, (z + 1) * line)) for z in range(LINES)],
    )
    kv = (gathered.astype(jnp.float32) * (1.0 / WEIGHT_SCALE)).astype(jnp.bfloat16)
    kv = kv.reshape(line, LINES, 2, kv_weight.shape[0], width)

    joined = attend(slots, block_band, latents, kv, null_key, null_value, out_weight)
    sent = (joined.astype(jnp.float32) * JOINED_SCALE).astype(jnp.float16)
    window = lax.all_gather(sent, "grp", axis=0, tiled=True)
    values = window.astype(jnp.float32) * (1.0 / JOINED_SCALE)
    center = values - jnp.mean(values, axis=-1, keepdims=True)
    spread = jnp.mean(center * center, axis=-1, keepdims=True)
    normed = (center * lax.rsqrt(spread + 1e-05) * mlp_gain).astype(jnp.bfloat16)
    hidden = jax.nn.gelu(jnp.dot(normed, up_rows, preferred_element_type=jnp.float32)).astype(
        jnp.bfloat16
    )
    me = lax.axis_index("grp")
    columns = width // groups

    def term(offset):
        owner = lax.rem(me + offset + groups, groups)
        rows = lax.dynamic_slice_in_dim(down_rows, owner * columns, columns, 0)
        return lax.optimization_barrier(
            lax.dot_general(
                hidden, rows, (((1,), (1,)), ((), ())), preferred_element_type=jnp.float32
            )
        )

    def hop(values, by):
        pairs = [(i, (i + by) % groups) for i in range(groups)]
        values = values.astype(jnp.bfloat16)
        return lax.ppermute(values, "grp", pairs)

    up_hops = groups // 2
    down_hops = groups - 1 - up_hops
    rising = hop(term(up_hops), 1)
    falling = hop(term(-down_hops), -1)
    for distance in range(1, up_hops):
        rising = hop(rising.astype(jnp.float32) + term(up_hops - distance), 1)
        if distance < down_hops:
            falling = hop(falling.astype(jnp.float32) + term(distance - down_hops), -1)
    residual = lax.dynamic_slice_in_dim(window, me * columns, columns, 1)
    total = term(0) + rising.astype(jnp.float32) + falling.astype(jnp.float32)
    return (residual.astype(jnp.float32) * (1.0 / JOINED_SCALE) + total).astype(jnp.bfloat16)


def solution(mesh):
    return jax.shard_map(
        local,
        mesh=mesh,
        in_specs=(
            P(("grp", "tm"), None),
            P(("grp", "tm"), None),
            P(("grp", "tm")),
            P(("grp", "tm")),
            P(("grp", "tm"), None),
            P("tm", None),
            P(),
            P(),
            P(),
            P(),
            P("tm", "grp"),
            P("grp", "tm"),
        ),
        out_specs=P("tm", "grp"),
        check_vma=False,
    )
```

```python
import jax
import jax.numpy as jnp
from jax import lax
from jax.experimental import pallas as pl
from jax.experimental.pallas import tpu as pltpu
from jax.sharding import PartitionSpec as P


HD = 128
BAND_LANES = 128
BAND_SHIFT = 4
WEIGHT_SCALE = 2.0**17
JOINED_SCALE = 0.25


def pack_kernel(owners, capacity, dest_ref, band_ref, rows_ref, out_ref):
    rows = rows_ref.shape[0]
    width = rows_ref.shape[1]
    slots = owners * capacity
    dest = dest_ref[...]
    owner_ids = lax.broadcasted_iota(jnp.int32, (owners, rows), 0)
    named = (owner_ids == dest).astype(jnp.float32)
    before = lax.broadcasted_iota(jnp.int32, (rows, rows), 0) < lax.broadcasted_iota(
        jnp.int32, (rows, rows), 1
    )
    earlier = jnp.dot(
        named.astype(jnp.bfloat16),
        before.astype(jnp.float32).astype(jnp.bfloat16),
        preferred_element_type=jnp.float32,
    )
    slot = jnp.sum(earlier * named, axis=0, keepdims=True).astype(jnp.int32)
    code = dest * capacity + slot
    chosen = lax.broadcasted_iota(jnp.int32, (slots, rows), 0) == code
    chosen_f = chosen.astype(jnp.float32)
    moved = jnp.dot(
        chosen_f.astype(jnp.bfloat16), rows_ref[...], preferred_element_type=jnp.float32
    )
    out_ref[:, :, :width] = moved.astype(jnp.bfloat16).reshape(owners, capacity, width)
    bands = jnp.sum(
        chosen_f * (band_ref[...] + BAND_SHIFT).astype(jnp.float32), axis=1, keepdims=True
    )
    out_ref[:, :, width:] = (
        jnp.broadcast_to(bands, (slots, BAND_LANES))
        .astype(jnp.bfloat16)
        .reshape(owners, capacity, BAND_LANES)
    )


def pack(audio_rows, destination, row_band, owners, capacity):
    rows, width = audio_rows.shape

    def body(*refs):
        pack_kernel(owners, capacity, *refs)

    return pl.pallas_call(
        body,
        out_shape=jax.ShapeDtypeStruct((owners, capacity, width + BAND_LANES), jnp.bfloat16),
        name="pack",
    )(destination.reshape(1, rows), row_band.reshape(1, rows), audio_rows)


def attend_kernel(
    band_ref,
    slots_ref,
    latents_ref,
    query_ref,
    wk_ref,
    wv_ref,
    nk_ref,
    nv_ref,
    wo_ref,
    out_ref,
    acc_ref,
    away_ref,
):
    step = pl.program_id(0)
    width = latents_ref.shape[1]
    slots = slots_ref.shape[0] * slots_ref.shape[1]
    scale = 1.0 / float(HD) ** 0.5

    @pl.when(step == 0)
    def _():
        acc_ref[...] = latents_ref[...].astype(jnp.float32)
        bands = slots_ref[:, :, width:].reshape(slots, BAND_LANES).astype(jnp.float32)
        here = (band_ref[0] + BAND_SHIFT).astype(jnp.float32)
        away_ref[...] = jnp.abs(jnp.transpose(bands) - here)

    frames = slots_ref[:, :, :width].reshape(slots, width)
    usable = away_ref[...] <= 1.0
    keys = jnp.dot(frames, wk_ref[...], preferred_element_type=jnp.float32).astype(jnp.bfloat16)
    values = jnp.dot(frames, wv_ref[...], preferred_element_type=jnp.float32).astype(jnp.bfloat16)
    attended = []
    for h in range(wk_ref.shape[1] // HD):
        cols = slice(h * HD, (h + 1) * HD)
        query = query_ref[:, cols]
        score = (
            lax.dot_general(
                query, keys[:, cols], (((1,), (1,)), ((), ())), preferred_element_type=jnp.float32
            )
            * scale
        )
        null = (
            jnp.sum(query.astype(jnp.float32) * nk_ref[:, cols], axis=1, keepdims=True) * scale
        )
        masked = jnp.where(usable, score, -1e30)
        highest = jnp.maximum(jnp.max(masked, axis=1, keepdims=True), null)
        expo = jnp.where(usable, jnp.exp(masked - highest), 0.0)
        null_expo = jnp.exp(null - highest)
        total = jnp.sum(expo, axis=1, keepdims=True) + null_expo
        inverse = 1.0 / total
        weights = (expo * inverse).astype(jnp.bfloat16)
        null_weight = (null_expo * inverse).astype(jnp.bfloat16).astype(jnp.float32)
        summed = jnp.dot(weights, values[:, cols], preferred_element_type=jnp.float32)
        attended.append((summed + null_weight * nv_ref[:, cols]).astype(jnp.bfloat16))
    acc_ref[...] += jnp.dot(
        jnp.concatenate(attended, axis=1), wo_ref[...], preferred_element_type=jnp.float32
    )

    @pl.when(step == pl.num_programs(0) - 1)
    def _():
        out_ref[...] = acc_ref[...].astype(jnp.bfloat16)


def attend(slots, block_band, latents, wk, wv, null_key, null_value, out_weight):
    count, width = latents.shape
    step = 4 * HD
    return pl.pallas_call(
        attend_kernel,
        grid=(width // step,),
        in_specs=[
            pl.BlockSpec(memory_space=pltpu.SMEM),
            pl.BlockSpec(slots.shape, lambda i: (0, 0, 0)),
            pl.BlockSpec((count, width), lambda i: (0, 0)),
            pl.BlockSpec((count, step), lambda i: (0, i)),
            pl.BlockSpec((width, step), lambda i: (0, i)),
            pl.BlockSpec((width, step), lambda i: (0, i)),
            pl.BlockSpec((1, step), lambda i: (0, i)),
            pl.BlockSpec((1, step), lambda i: (0, i)),
            pl.BlockSpec((step, width), lambda i: (i, 0)),
        ],
        out_specs=pl.BlockSpec((count, width), lambda i: (0, 0)),
        out_shape=jax.ShapeDtypeStruct((count, width), jnp.bfloat16),
        scratch_shapes=[
            pltpu.VMEM((count, width), jnp.float32),
            pltpu.VMEM((count, slots.shape[0] * slots.shape[1]), jnp.float32),
        ],
        compiler_params=pltpu.CompilerParams(vmem_limit_bytes=52 << 20),
        name="attend",
    )(
        block_band,
        slots,
        latents,
        latents,
        wk,
        wv,
        null_key.reshape(1, width),
        null_value.reshape(1, width),
        out_weight,
    )


def local(
    audio_rows,
    routing,
    row_band,
    block_band,
    latents,
    kv_weight,
    null_key,
    null_value,
    out_weight,
    mlp_gain,
    up_weight,
    down_weight,
):
    local_rows = audio_rows.shape[0]
    width = latents.shape[1]
    owners = lax.axis_size("tm")
    groups = lax.axis_size("grp")
    capacity = max(2, 2 * local_rows // owners)

    payload = pack(audio_rows, routing[:, 0], row_band, owners, capacity)
    slots = lax.all_to_all(payload, "tm", split_axis=0, concat_axis=0, tiled=True)

    shard = jnp.concatenate(
        [kv_weight[:, :width], kv_weight[:, width:], up_weight, jnp.transpose(down_weight)], axis=0
    )
    shard = (shard.astype(jnp.float32) * WEIGHT_SCALE).astype(jnp.float16)
    gathered = lax.all_gather(shard, "tm", axis=0, tiled=True)
    gathered = gathered.reshape(owners, 4, kv_weight.shape[0], width)

    def whole(index):
        part = gathered[:, index].astype(jnp.float32) * (1.0 / WEIGHT_SCALE)
        return part.astype(jnp.bfloat16).reshape(width, width)

    joined = attend(
        slots, block_band, latents, whole(0), whole(1), null_key, null_value, out_weight
    )
    sent = (joined.astype(jnp.float32) * JOINED_SCALE).astype(jnp.float16)
    window = lax.all_gather(sent, "grp", axis=0, tiled=True)
    values = window.astype(jnp.float32) * (1.0 / JOINED_SCALE)
    center = values - jnp.mean(values, axis=-1, keepdims=True)
    spread = jnp.mean(center * center, axis=-1, keepdims=True)
    normed = (center * lax.rsqrt(spread + 1e-05) * mlp_gain).astype(jnp.bfloat16)
    hidden = jax.nn.gelu(jnp.dot(normed, whole(2), preferred_element_type=jnp.float32)).astype(
        jnp.bfloat16
    )
    down_rows = whole(3)
    me = lax.axis_index("grp")
    columns = width // groups
    way = 1 - 2 * lax.rem(lax.axis_index("tm"), 2)

    def term(offset):
        owner = lax.rem(me + way * offset + groups, groups)
        rows = lax.dynamic_slice_in_dim(down_rows, owner * columns, columns, 0)
        value = lax.dot_general(
            hidden, rows, (((1,), (1,)), ((), ())), preferred_element_type=jnp.float32
        )
        return lax.optimization_barrier(value)

    def hop(values, by):
        pairs = []
        for group in range(groups):
            for place in range(owners):
                target = (group + (by if place % 2 == 0 else -by)) % groups
                pairs.append((group * owners + place, target * owners + place))
        values = values.astype(jnp.bfloat16)
        return lax.ppermute(values, ("grp", "tm"), pairs)

    up_hops = groups // 2
    down_hops = groups - 1 - up_hops
    rising = hop(term(up_hops), 1)
    falling = hop(term(-down_hops), -1)
    for distance in range(1, up_hops):
        rising = hop(rising.astype(jnp.float32) + term(up_hops - distance), 1)
        if distance < down_hops:
            falling = hop(falling.astype(jnp.float32) + term(distance - down_hops), -1)
    residual = lax.dynamic_slice_in_dim(window, me * columns, columns, 1)
    total = term(0) + rising.astype(jnp.float32) + falling.astype(jnp.float32)
    return (residual.astype(jnp.float32) * (1.0 / JOINED_SCALE) + total).astype(jnp.bfloat16)


def solution(mesh):
    return jax.shard_map(
        local,
        mesh=mesh,
        in_specs=(
            P(("grp", "tm"), None),
            P(("grp", "tm"), None),
            P(("grp", "tm")),
            P(("grp", "tm")),
            P(("grp", "tm"), None),
            P("tm", None),
            P(),
            P(),
            P(),
            P(),
            P("tm", "grp"),
            P("grp", "tm"),
        ),
        out_specs=P("tm", "grp"),
        check_vma=False,
    )
```

```python
import jax
import jax.numpy as jnp
from jax import lax
from jax.experimental import pallas as pl
from jax.experimental.pallas import tpu as pltpu
from jax.sharding import PartitionSpec as P


HD = 128
BAND_LANES = 128
BAND_SHIFT = 4
WEIGHT_SCALE = 2.0**17
JOINED_SCALE = 0.25


def pack_kernel(owners, capacity, dest_ref, band_ref, rows_ref, out_ref):
    rows = rows_ref.shape[0]
    width = rows_ref.shape[1]
    slots = owners * capacity
    dest = dest_ref[...]
    owner_ids = lax.broadcasted_iota(jnp.int32, (owners, rows), 0)
    named = (owner_ids == dest).astype(jnp.float32)
    before = lax.broadcasted_iota(jnp.int32, (rows, rows), 0) < lax.broadcasted_iota(
        jnp.int32, (rows, rows), 1
    )
    earlier = jnp.dot(
        named.astype(jnp.bfloat16),
        before.astype(jnp.float32).astype(jnp.bfloat16),
        preferred_element_type=jnp.float32,
    )
    slot = jnp.sum(earlier * named, axis=0, keepdims=True).astype(jnp.int32)
    code = dest * capacity + slot
    chosen = lax.broadcasted_iota(jnp.int32, (slots, rows), 0) == code
    chosen_f = chosen.astype(jnp.float32)
    moved = jnp.dot(
        chosen_f.astype(jnp.bfloat16), rows_ref[...], preferred_element_type=jnp.float32
    )
    out_ref[:, :, :width] = moved.astype(jnp.bfloat16).reshape(owners, capacity, width)
    bands = jnp.sum(
        chosen_f * (band_ref[...] + BAND_SHIFT).astype(jnp.float32), axis=1, keepdims=True
    )
    out_ref[:, :, width:] = (
        jnp.broadcast_to(bands, (slots, BAND_LANES))
        .astype(jnp.bfloat16)
        .reshape(owners, capacity, BAND_LANES)
    )


def pack(audio_rows, destination, row_band, owners, capacity):
    rows, width = audio_rows.shape

    def body(*refs):
        pack_kernel(owners, capacity, *refs)

    return pl.pallas_call(
        body,
        out_shape=jax.ShapeDtypeStruct((owners, capacity, width + BAND_LANES), jnp.bfloat16),
        name="pack",
    )(destination.reshape(1, rows), row_band.reshape(1, rows), audio_rows)


def attend_kernel(
    band_ref,
    slots_ref,
    latents_ref,
    query_ref,
    wk_ref,
    wv_ref,
    nk_ref,
    nv_ref,
    wo_ref,
    out_ref,
    acc_ref,
    away_ref,
):
    step = pl.program_id(0)
    width = latents_ref.shape[1]
    slots = slots_ref.shape[0] * slots_ref.shape[1]
    scale = 1.0 / float(HD) ** 0.5

    @pl.when(step == 0)
    def _():
        acc_ref[...] = latents_ref[...].astype(jnp.float32)
        bands = slots_ref[:, :, width:].reshape(slots, BAND_LANES).astype(jnp.float32)
        here = (band_ref[0] + BAND_SHIFT).astype(jnp.float32)
        away_ref[...] = jnp.abs(jnp.transpose(bands) - here)

    frames = slots_ref[:, :, :width].reshape(slots, width)
    usable = away_ref[...] <= 1.0
    keys = jnp.dot(frames, wk_ref[...], preferred_element_type=jnp.float32).astype(jnp.bfloat16)
    values = jnp.dot(frames, wv_ref[...], preferred_element_type=jnp.float32).astype(jnp.bfloat16)
    attended = []
    for h in range(wk_ref.shape[1] // HD):
        cols = slice(h * HD, (h + 1) * HD)
        query = query_ref[:, cols]
        score = (
            lax.dot_general(
                query, keys[:, cols], (((1,), (1,)), ((), ())), preferred_element_type=jnp.float32
            )
            * scale
        )
        null = (
            jnp.sum(query.astype(jnp.float32) * nk_ref[:, cols], axis=1, keepdims=True) * scale
        )
        masked = jnp.where(usable, score, -1e30)
        highest = jnp.maximum(jnp.max(masked, axis=1, keepdims=True), null)
        expo = jnp.where(usable, jnp.exp(masked - highest), 0.0)
        null_expo = jnp.exp(null - highest)
        total = jnp.sum(expo, axis=1, keepdims=True) + null_expo
        inverse = 1.0 / total
        weights = (expo * inverse).astype(jnp.bfloat16)
        null_weight = (null_expo * inverse).astype(jnp.bfloat16).astype(jnp.float32)
        summed = jnp.dot(weights, values[:, cols], preferred_element_type=jnp.float32)
        attended.append((summed + null_weight * nv_ref[:, cols]).astype(jnp.bfloat16))
    acc_ref[...] += jnp.dot(
        jnp.concatenate(attended, axis=1), wo_ref[...], preferred_element_type=jnp.float32
    )

    @pl.when(step == pl.num_programs(0) - 1)
    def _():
        out_ref[...] = acc_ref[...].astype(jnp.bfloat16)


def attend(slots, block_band, latents, wk, wv, null_key, null_value, out_weight):
    count, width = latents.shape
    step = 4 * HD
    return pl.pallas_call(
        attend_kernel,
        grid=(width // step,),
        in_specs=[
            pl.BlockSpec(memory_space=pltpu.SMEM),
            pl.BlockSpec(slots.shape, lambda i: (0, 0, 0)),
            pl.BlockSpec((count, width), lambda i: (0, 0)),
            pl.BlockSpec((count, step), lambda i: (0, i)),
            pl.BlockSpec((width, step), lambda i: (0, i)),
            pl.BlockSpec((width, step), lambda i: (0, i)),
            pl.BlockSpec((1, step), lambda i: (0, i)),
            pl.BlockSpec((1, step), lambda i: (0, i)),
            pl.BlockSpec((step, width), lambda i: (i, 0)),
        ],
        out_specs=pl.BlockSpec((count, width), lambda i: (0, 0)),
        out_shape=jax.ShapeDtypeStruct((count, width), jnp.bfloat16),
        scratch_shapes=[
            pltpu.VMEM((count, width), jnp.float32),
            pltpu.VMEM((count, slots.shape[0] * slots.shape[1]), jnp.float32),
        ],
        compiler_params=pltpu.CompilerParams(vmem_limit_bytes=49 << 20),
        name="attend",
    )(
        block_band,
        slots,
        latents,
        latents,
        wk,
        wv,
        null_key.reshape(1, width),
        null_value.reshape(1, width),
        out_weight,
    )


def local(
    audio_rows,
    routing,
    row_band,
    block_band,
    latents,
    kv_weight,
    null_key,
    null_value,
    out_weight,
    mlp_gain,
    up_weight,
    down_weight,
):
    local_rows = audio_rows.shape[0]
    width = latents.shape[1]
    owners = lax.axis_size("tm")
    groups = lax.axis_size("grp")
    capacity = max(2, 2 * local_rows // owners)

    payload = pack(audio_rows, routing[:, 0], row_band, owners, capacity)
    slots = lax.all_to_all(payload, "tm", split_axis=0, concat_axis=0, tiled=True)

    shard = jnp.concatenate(
        [kv_weight[:, :width], kv_weight[:, width:], up_weight, jnp.transpose(down_weight)], axis=0
    )
    shard = (shard.astype(jnp.float32) * WEIGHT_SCALE).astype(jnp.float16)
    gathered = lax.all_gather(shard, "tm", axis=0, tiled=True)
    gathered = gathered.reshape(owners, 4, kv_weight.shape[0], width)

    def whole(index):
        part = gathered[:, index].astype(jnp.float32) * (1.0 / WEIGHT_SCALE)
        return part.astype(jnp.bfloat16).reshape(width, width)

    joined = attend(
        slots, block_band, latents, whole(0), whole(1), null_key, null_value, out_weight
    )
    sent = (joined.astype(jnp.float32) * JOINED_SCALE).astype(jnp.float16)
    window = lax.all_gather(sent, "grp", axis=0, tiled=True)
    values = window.astype(jnp.float32) * (1.0 / JOINED_SCALE)
    center = values - jnp.mean(values, axis=-1, keepdims=True)
    spread = jnp.mean(center * center, axis=-1, keepdims=True)
    normed = (center * lax.rsqrt(spread + 1e-05) * mlp_gain).astype(jnp.bfloat16)
    hidden = jax.nn.gelu(jnp.dot(normed, whole(2), preferred_element_type=jnp.float32)).astype(
        jnp.bfloat16
    )
    down_rows = whole(3)
    me = lax.axis_index("grp")
    columns = width // groups

    def term(offset):
        owner = lax.rem(me + offset + groups, groups)
        rows = lax.dynamic_slice_in_dim(down_rows, owner * columns, columns, 0)
        value = lax.dot_general(
            hidden, rows, (((1,), (1,)), ((), ())), preferred_element_type=jnp.float32
        )
        return lax.optimization_barrier(value)

    def hop(values, by):
        pairs = [(i, (i + by) % groups) for i in range(groups)]
        values = values.astype(jnp.bfloat16)
        return lax.ppermute(values, "grp", pairs)

    up_hops = groups // 2
    down_hops = groups - 1 - up_hops
    rising = hop(term(up_hops), 1)
    falling = hop(term(-down_hops), -1)
    for distance in range(1, up_hops):
        rising = hop(rising.astype(jnp.float32) + term(up_hops - distance), 1)
        if distance < down_hops:
            falling = hop(falling.astype(jnp.float32) + term(distance - down_hops), -1)
    residual = lax.dynamic_slice_in_dim(window, me * columns, columns, 1)
    total = term(0) + rising.astype(jnp.float32) + falling.astype(jnp.float32)
    return (residual.astype(jnp.float32) * (1.0 / JOINED_SCALE) + total).astype(jnp.bfloat16)


def solution(mesh):
    return jax.shard_map(
        local,
        mesh=mesh,
        in_specs=(
            P(("grp", "tm"), None),
            P(("grp", "tm"), None),
            P(("grp", "tm")),
            P(("grp", "tm")),
            P(("grp", "tm"), None),
            P("tm", None),
            P(),
            P(),
            P(),
            P(),
            P("tm", "grp"),
            P("grp", "tm"),
        ),
        out_specs=P("tm", "grp"),
        check_vma=False,
    )
```
